32 devices in a mesh: dp: 4 (over x, core), expert: 8 (over z, y).
Axes of the slice: x: 2, y: 2, z: 4, core: 2. Of those that a mesh axis runs over, the one named last changes fastest.
Arguments:
- tokens: bfloat16 [4, 2048, 768], P('dp', 'expert'), may hold values from -6 to 6
- routes: int32 [4, 2048, 2], P('dp', 'expert'), may hold values from 0 to 11, all different within a row; in each aligned block of 256 rows (0 to 255, 256 to 511, ..., all dimensions but the last counted through in order) at most 64 rows name the same one
- pieces: int32 [4, 3], P('dp'), may hold values from 0 to 1792, as said below
- prev_logits: float32 [4, 2048, 12], P('dp', 'expert'), may hold values from -5 to 5
- cotangent: bfloat16 [4, 2048, 768], P('dp', 'expert'), may hold values from -6 to 6
- first_gain: float32 [768], replicated, may hold values from 0.5 to 1.5
- query_weight: bfloat16 [768, 768], replicated
- key_weight: bfloat16 [768, 768], replicated, may hold values from -0.21875 to 0.21875
- value_weight: bfloat16 [768, 768], replicated, may hold values from -0.21875 to 0.21875
- out_weight: bfloat16 [768, 768], replicated, may hold values from -1.75 to 1.75
- second_gain: float32 [768], replicated, may hold values from 0.5 to 1.5
- router_weight: bfloat16 [768, 12], replicated, may hold values from -0.14941406 to 0.14941406
- gate_mix: float32 [12, 12], replicated, may hold values from -0.9 to 0.9
- const_mixer: bfloat16 [2, 2, 768], replicated, may hold values from -0.21875 to 0.21875
- const_vector: float32 [2, 768], replicated, may hold values from -6 to 6
- expert_gate: bfloat16 [8, 768, 2048], P('expert'), may hold values from -0.21875 to 0.21875
- expert_up: bfloat16 [8, 768, 2048], P('expert'), may hold values from -0.21875 to 0.21875
- expert_down: bfloat16 [8, 2048, 768], P('expert'), may hold values from -0.1875 to 0.1875
Outputs:
- output: bfloat16 [4, 2048, 768], P('dp', 'expert')
- input_grad: float32 [4, 2048, 768], P('dp', 'expert')
- prev_grad: float32 [4, 2048, 12], P('dp', 'expert')
- first_gain_grad: float32 [768], P(('dp', 'expert'))
- query_grad: float32 [768, 768], P(('dp', 'expert'))
- key_grad: float32 [768, 768], P(('dp', 'expert'))
- value_grad: float32 [768, 768], P(('dp', 'expert'))
- out_grad: float32 [768, 768], P(('dp', 'expert'))
- second_gain_grad: float32 [768], P(('dp', 'expert'))
- router_grad: float32 [768, 12], P(('dp', 'expert'))
- mix_grad: float32 [12, 12], replicated
- const_mixer_grad: float32 [2, 2, 768], P(None, None, ('dp', 'expert'))
- const_vector_grad: float32 [2, 768], P(None, ('dp', 'expert'))
- expert_gate_grad: float32 [8, 768, 2048], P('expert', 'dp')
- expert_up_grad: float32 [8, 768, 2048], P('expert', 'dp')
- expert_down_grad: float32 [8, 2048, 768], P('expert', 'dp')
- clipped_query: bfloat16 [768, 768], replicated
- clipped_key: bfloat16 [768, 768], replicated
- clip_factors: float32 [12], replicated
The draws below stay inside these ranges and needn't reach their ends.
Inputs may be any that keep to these rules, and one draw needn't show every extreme that they name: `routes`: each row names two different targets; in each aligned block of 256 rows (one sequence's rows on one index of expert) no target is named by more than 64 rows, a bound that some block reaches. Within a sequence the starts ascend and the pieces of 256 tokens do not intersect.
All inputs are finite; a program needn't handle non-finite values.
Results may differ from the reference program's by a relative error of at most 0.015.
Values may be sent and summed in bfloat16 or wider, within the bound.
No kernel may reach another device: no remote copies, remote signals or barrier semaphores. Data moves between devices by JAX's collectives and lax.ppermute only.
A program may use at most 192 MiB of HBM per device.

```python
import math
import jax
import jax.numpy as jnp
import numpy as np
from jax import lax

D = 768
HEADS = 12
HDIM = 64
FF = 2048
EXPERTS = 8
CONSTS = 2
SEQ = 2048
PIECE = 256
PICS = 3
NE = 12
SEQS = 4
SEQ_DEV = 256
MOST = 64
N_EXPERT = 8


def draw_pieces(key, part):
    region = SEQ // PICS
    offsets = jax.random.randint(key, (SEQS, PICS), 0, region - PIECE + 1, dtype=jnp.int32)
    return offsets + jnp.arange(PICS, dtype=jnp.int32)[None, :] * region


def draw_query_weight(key, part):
    scale_key, entry_key = jax.random.split(key)
    head_scale = jnp.exp(jax.random.uniform(scale_key, (HEADS,), jnp.float32, math.log(0.9), math.log(2.2)))
    entries = jax.random.normal(entry_key, (D, D), jnp.float32)
    return (entries * D ** (-0.5) * jnp.repeat(head_scale, HDIM)[None, :]).astype(jnp.bfloat16)


def shard_levels(key, dims, shards, low, high):
    def one(dim, parts):
        draws = jax.random.uniform(jax.random.fold_in(jax.random.fold_in(key, 6), dim), (parts,), jnp.float32, low / len(shards), high / len(shards))
        return jnp.repeat(jnp.exp(draws), dims[dim] // parts).reshape((-1,) + (1,) * (len(dims) - dim - 1))

    factor_of = one(*shards[0])
    for cut in shards[1:]:
        factor_of = factor_of * one(*cut)
    return factor_of


def deal_out(own_key, own, number, rows, count, top, reach, lean):
    order = jax.random.permutation(own_key, count)
    packed, common = load_shares(count, rows * top, reach, lean, True), load_shares(count, rows * top, reach, lean, False)
    places = jnp.arange(count)

    def named(lengths, offset_by):
        used = int((lengths > 0).sum())
        fixed = max(1, used // 4)
        shifted = fixed + (places - fixed + offset_by * (used - fixed)) % max(1, count - fixed)
        return jnp.zeros((count,), jnp.int32).at[order[jnp.where(places < fixed, places, shifted)]].set(jnp.asarray(lengths, jnp.int32))

    lengths = jnp.where(number % 4 == 0, named(packed, number // 4), named(common, number - number // 4 - 1))
    mixed = jax.random.permutation(jax.random.fold_in(own, 3), count)
    source_of, receiver = mixed[0:count // 2 * 2:2], mixed[1:count // 2 * 2:2]
    slack = jnp.minimum(lengths[source_of] - 1, reach - lengths[receiver]) // 2
    slack = jnp.where((source_of == order[0]) | (receiver == order[0]) | (lengths[receiver] == 0), 0, jnp.maximum(slack, 0))
    shifted = jax.random.randint(jax.random.fold_in(own, 4), (count // 2,), 0, 1 << 20) % (slack + 1)
    lengths = lengths.at[source_of].add(-shifted).at[receiver].add(shifted)
    items = jnp.searchsorted(jnp.cumsum(lengths), jnp.arange(rows * top), side="right").astype(jnp.int32)
    listing = items.reshape(top, rows).T
    listing = listing[jax.random.permutation(jax.random.fold_in(own, 1), rows)]
    offset_by = jax.random.randint(jax.random.fold_in(own, 2), (rows, 1), 0, top)
    return jnp.take_along_axis(listing, (jnp.arange(top)[None, :] + offset_by) % top, axis=1)


def load_shares(amount, total, most, skew, full):
    loads = [(1 << 20) // math.isqrt(rank ** skew) + 1 for rank in range(1, amount + 1)]
    largest = most if full else min(most, max(-(-total // amount), total * loads[0] // sum(loads)))
    least = 1 if total - largest >= amount - 1 else 0
    given, surplus = [largest] + [least] * (amount - 1), total - largest - least * (amount - 1)
    while surplus > 0:
        candidates = [i for i in range(1, amount) if given[i] < largest] or [i for i in range(1, amount) if given[i] < most]
        mass, remaining = sum([loads[i] for i in candidates]), surplus
        for i in candidates:
            extra = min(most - given[i], max(1, remaining * loads[i] // mass), surplus)
            given[i] = given[i] + extra
            surplus = surplus - extra
    return np.array(given)


def centred(stream_key, shape, width, limit, shards=(), kind=jnp.bfloat16):
    drawn = jax.random.normal(stream_key, shape, jnp.float32) * width
    if len(shards) > 0:
        drawn = shard_levels(stream_key, shape, shards, -0.22, 0.18) * drawn
    return jnp.clip(drawn, min=-limit, max=limit).astype(kind)


def setup_inputs(seed: int = 0) -> dict:
    arg_keys = jax.random.split(jax.random.key(seed), 19)
    tokens = centred(arg_keys[0], (SEQS, SEQ, D), 1.0, 6.0, ((0, 4), (1, 8)))
    routes_keys = jax.random.split(jax.random.fold_in(arg_keys[1], 1), SEQS * SEQ // SEQ_DEV)
    routes_turns = jax.random.permutation(jax.random.fold_in(arg_keys[1], 3), SEQS * SEQ // SEQ_DEV)
    routes = jax.vmap(lambda own, number: deal_out(jax.random.fold_in(arg_keys[1], 2), own, number, SEQ_DEV, NE, 2, MOST, 2))(routes_keys, routes_turns).reshape((SEQS, SEQ, 2))
    pieces = draw_pieces(jax.random.fold_in(arg_keys[18], 71), 0)
    prev_logits = centred(arg_keys[3], (SEQS, SEQ, NE), 0.8, 5.0, ((0, 4), (1, 8)), jnp.float32)
    cotangent = centred(arg_keys[4], (SEQS, SEQ, D), 1.0, 6.0, ((0, 4), (1, 8)))
    first_gain = jnp.clip(1.0 + 0.1 * jax.random.normal(arg_keys[5], (D,), jnp.float32), 0.5, 1.5)
    query_weight = draw_query_weight(jax.random.fold_in(arg_keys[18], 71), 0)
    key_weight = centred(arg_keys[7], (D, D), D ** -0.5, 0.21875)
    value_weight = centred(arg_keys[8], (D, D), D ** -0.5, 0.21875)
    out_weight = centred(arg_keys[9], (D, D), (D // 64) ** -0.5, 1.75)
    second_gain = jnp.clip(1.0 + 0.1 * jax.random.normal(arg_keys[10], (D,), jnp.float32), 0.5, 1.5)
    router_weight = centred(arg_keys[11], (D, NE), 0.025, 0.14941406)
    gate_mix = centred(arg_keys[12], (NE, NE), 0.15, 0.9, (), jnp.float32)
    const_mixer = centred(arg_keys[13], (CONSTS, 2, D), D ** -0.5, 0.21875)
    const_vector = centred(arg_keys[14], (CONSTS, D), 1.0, 6.0, (), jnp.float32)
    expert_gate = centred(arg_keys[15], (EXPERTS, D, FF), D ** -0.5, 0.21875, ((0, 8),))
    expert_up = centred(arg_keys[16], (EXPERTS, D, FF), D ** -0.5, 0.21875, ((0, 8),))
    expert_down = centred(arg_keys[17], (EXPERTS, FF, D), (FF // 2) ** -0.5, 0.1875, ((0, 8),))
    return {"tokens": tokens, "routes": routes, "pieces": pieces, "prev_logits": prev_logits, "cotangent": cotangent, "first_gain": first_gain, "query_weight": query_weight, "key_weight": key_weight, "value_weight": value_weight, "out_weight": out_weight, "second_gain": second_gain, "router_weight": router_weight, "gate_mix": gate_mix, "const_mixer": const_mixer, "const_vector": const_vector, "expert_gate": expert_gate, "expert_up": expert_up, "expert_down": expert_down}


@jax.custom_vjp
def low(v):
    return lax.optimization_barrier(v.astype(jnp.bfloat16)).astype(jnp.float32)

@jax.custom_vjp
def low_back(v):
    return v

def low_keep(v):
    return (low(v), None)

def low_pass(kept, grad):
    return (grad,)

def back_keep(v):
    return (v, None)

def back_low(kept, grad):
    return (low(grad),)
low.defvjp(low_keep, low_pass)
low_back.defvjp(back_keep, back_low)
EPSILON = 1e-06
CLIP_LIMIT = 2.0
NEGATIVE_FILL = -1e+30
HIGHEST = lax.Precision.HIGHEST

def as_float(values):
    return values.astype(jnp.float32)

def rms_norm(values, gain):
    return values * lax.rsqrt(lax.optimization_barrier(jnp.mean(values * values, axis=-1, keepdims=True)) + EPSILON) * gain

def one_sequence(params, data):
    first_gain, query_weight, key_weight, value_weight, out_weight, second_gain, router_weight, gate_mix, const_mixer, const_vector, expert_gate, expert_up, expert_down = params
    inputs, previous, route_ids, starts = data
    positions = jnp.arange(SEQ, dtype=jnp.int32)
    inside = (positions[:, None] >= starts[None, :]) & (positions[:, None] < starts[None, :] + PIECE)
    labels = lax.optimization_barrier(jnp.sum(jnp.where(inside, jnp.arange(1, PICS + 1, dtype=jnp.int32)[None, :], 0), axis=1))
    allowed = (positions[None, :] <= positions[:, None]) | (labels[:, None] == labels[None, :]) & (labels[:, None] > 0)
    first_low = low(rms_norm(inputs, first_gain))
    queries = low(low_back(jnp.dot(first_low, query_weight, precision=HIGHEST)))
    key_rows = low(low_back(jnp.dot(first_low, key_weight, precision=HIGHEST)))
    value_rows = low(low_back(jnp.dot(first_low, value_weight, precision=HIGHEST)))
    query_heads = queries.reshape(SEQ, HEADS, HDIM)
    key_heads = key_rows.reshape(SEQ, HEADS, HDIM)
    value_heads = value_rows.reshape(SEQ, HEADS, HDIM)
    scores = low_back(jnp.einsum('qhd,khd->hqk', query_heads, key_heads, precision=HIGHEST) * 0.125)
    scores = jnp.where(allowed[None], scores, NEGATIVE_FILL)
    top_score = lax.optimization_barrier(jnp.max(scores, axis=(1, 2)))
    attend = jax.nn.softmax(scores, axis=-1)
    context = jnp.einsum('hqk,khd->qhd', low(attend), value_heads, precision=HIGHEST).reshape(SEQ, D)
    context = low(low_back(context))
    middle = inputs + low_back(jnp.dot(context, out_weight, precision=HIGHEST))
    second_low = low(rms_norm(middle, second_gain))
    logits = jnp.dot(second_low, router_weight, precision=HIGHEST) + jnp.dot(previous, gate_mix, precision=HIGHEST)
    probabilities = jax.nn.softmax(logits, axis=-1)
    picked = jnp.take_along_axis(probabilities, route_ids, axis=1)
    shares = picked / lax.optimization_barrier(jnp.sum(picked, axis=1, keepdims=True))
    flat_ids = route_ids.reshape(-1)
    token_of = jnp.arange(2 * SEQ, dtype=jnp.int32) // 2
    route_in = low_back(second_low[token_of])
    routed = jnp.zeros((2 * SEQ, D), jnp.float32)
    capacity = MOST * N_EXPERT
    for expert_index in range(EXPERTS):
        order = jnp.argsort(jnp.where(flat_ids == expert_index, 0, 1).astype(jnp.int32))[:capacity]
        valid = (flat_ids[order] == expert_index).astype(jnp.float32)[:, None]
        rows_in = route_in[order]
        gate_act = low_back(jnp.dot(rows_in, expert_gate[expert_index], precision=HIGHEST))
        up_act = low_back(jnp.dot(rows_in, expert_up[expert_index], precision=HIGHEST))
        hidden = low(jax.nn.silu(gate_act) * up_act)
        result = low_back(low(jnp.dot(hidden, expert_down[expert_index], precision=HIGHEST)))
        routed = routed.at[order].add(result * valid)
    routed = routed.reshape(SEQ, 2, D)
    mixer = jax.nn.softmax(jnp.einsum('td,cjd->tcj', second_low, const_mixer, precision=HIGHEST), axis=-1)
    const_out = mixer[:, :, :1] * second_low[:, None, :] + mixer[:, :, 1:] * const_vector[None]
    mixture = jnp.zeros((SEQ, D), jnp.float32)
    for route_slot in range(2):
        target = route_ids[:, route_slot:route_slot + 1]
        branch = routed[:, route_slot] + jnp.where(target == EXPERTS + 1, second_low, 0.0)
        for const_index in range(CONSTS):
            branch = branch + jnp.where(target == EXPERTS + 2 + const_index, const_out[:, const_index], 0.0)
        mixture = mixture + shares[:, route_slot:route_slot + 1] * branch
    return (middle + mixture, top_score)

def reference(tokens, routes, pieces, prev_logits, cotangent, first_gain, query_weight, key_weight, value_weight, out_weight, second_gain, router_weight, gate_mix, const_mixer, const_vector, expert_gate, expert_up, expert_down):
    params = tuple((as_float(weight_item) for weight_item in (first_gain, query_weight, key_weight, value_weight, out_weight, second_gain, router_weight, gate_mix, const_mixer, const_vector, expert_gate, expert_up, expert_down)))

    def forward(inputs, previous, weights):

        def one_step(data):
            return one_sequence(weights, data)
        results, tops = lax.map(jax.checkpoint(one_step), (inputs, previous, routes, pieces))
        return (results, lax.optimization_barrier(jnp.max(tops, axis=0)))
    result, pullback, top_score = jax.vjp(forward, as_float(tokens), prev_logits, params, has_aux=True)
    input_grad, prev_grad, grads = pullback(as_float(cotangent))
    factors = jnp.minimum(1.0, CLIP_LIMIT / top_score)
    root = jnp.repeat(jnp.sqrt(factors), HDIM)
    clipped_query = (as_float(query_weight) * root[None, :]).astype(jnp.bfloat16)
    clipped_key = (as_float(key_weight) * root[None, :]).astype(jnp.bfloat16)
    return (result.astype(jnp.bfloat16), input_grad, prev_grad, grads[0], grads[1], grads[2], grads[3], grads[4], grads[5], grads[6], grads[7], grads[8], grads[9], grads[10], grads[11], grads[12], clipped_query, clipped_key, factors)
```

```python
import functools

import jax
import jax.numpy as jnp
from jax import lax
from jax.experimental import pallas as pl
from jax.experimental.pallas import tpu as pltpu
from jax.sharding import PartitionSpec as P

HEADS = 12
HDIM = 64
EXPERTS = 8
PIECE = 256
EPSILON = 1e-06
CLIP_LIMIT = 2.0
NEGATIVE_FILL = -1e30
HIGHEST = lax.Precision.HIGHEST
LANES = 128
F32 = jnp.float32
BF16 = jnp.bfloat16
VMEM_BYTES = 60 * 1024 * 1024
QT = 256
KT = 512


def dot_nn(a, b, precision=None):
    return lax.dot_general(
        a, b, (((1,), (0,)), ((), ())), preferred_element_type=F32, precision=precision
    )


def dot_nt(a, b, precision=None):
    return lax.dot_general(
        a, b, (((1,), (1,)), ((), ())), preferred_element_type=F32, precision=precision
    )


def dot_tn(a, b, precision=None):
    return lax.dot_general(
        a, b, (((0,), (0,)), ((), ())), preferred_element_type=F32, precision=precision
    )


def head_start(index):
    return (index // 2) * 3 * HDIM + (index % 2) * HDIM


def call(body, out_shape, *args, scratch=(), smem=(), flops=0):
    vmem = pl.BlockSpec(memory_space=pltpu.VMEM)
    specs = [
        pl.BlockSpec(memory_space=pltpu.SMEM) if i in smem else vmem for i in range(len(args))
    ]
    outs = jax.tree.leaves(out_shape)
    nbytes = sum(a.size * a.dtype.itemsize for a in list(args) + outs)
    return pl.pallas_call(
        body,
        out_shape=out_shape,
        in_specs=specs,
        out_specs=jax.tree.map(lambda _: vmem, out_shape),
        scratch_shapes=list(scratch),
        compiler_params=pltpu.CompilerParams(vmem_limit_bytes=VMEM_BYTES),
        cost_estimate=pl.CostEstimate(flops=flops, bytes_accessed=nbytes, transcendentals=0),
    )(*args)


def struct(shape, dtype):
    return jax.ShapeDtypeStruct(shape, dtype)


def project_kernel(tokens, gain, wq, wk, wv, first_low, send):
    x = tokens[...].astype(F32)
    scale = lax.rsqrt(jnp.mean(x * x, axis=-1, keepdims=True) + EPSILON)
    low = (x * scale * gain[...]).astype(BF16)
    first_low[...] = low
    for part, weight in enumerate((wq, wk, wv)):
        full = dot_nn(low, weight[...])
        for index in range(send.shape[0]):
            start = head_start(index)
            send[index, :, part * LANES : (part + 1) * LANES] = full[
                :, start : start + LANES
            ].astype(BF16)


def route_kernel(routes, prev, mix, dy, dispatch, first_t, second_t, info, hits, dy_send):
    rows = routes.shape[0]
    slots = dispatch.shape[0]
    most = slots // EXPERTS
    lane = lax.broadcasted_iota(jnp.int32, (rows, LANES), 1)
    ids = routes[...]
    hit1 = (ids[:, 0:1] == lane).astype(F32)
    hit2 = (ids[:, 1:2] == lane).astype(F32)
    before = (
        lax.broadcasted_iota(jnp.int32, (rows, rows), 1)
        < lax.broadcasted_iota(jnp.int32, (rows, rows), 0)
    ).astype(F32)
    rank = dot_nn(before.astype(BF16), (hit1 + hit2).astype(BF16))
    spread = (
        lax.broadcasted_iota(jnp.int32, (LANES, slots), 0)
        == lax.broadcasted_iota(jnp.int32, (LANES, slots), 1) // most
    ).astype(F32).astype(BF16)
    place = (lax.broadcasted_iota(jnp.int32, (rows, slots), 1) % most).astype(F32)
    here = (dot_nn(rank.astype(BF16), spread) == place).astype(F32)
    one = here * dot_nn(hit1.astype(BF16), spread)
    two = here * dot_nn(hit2.astype(BF16), spread)
    first_t[...] = one.astype(BF16)
    second_t[...] = two.astype(BF16)
    table = (one + two).T.astype(BF16)
    signed = (one - two).T.astype(BF16)
    dispatch[...] = table
    mixed = dot_nn(prev[...], mix[...], HIGHEST)
    gap = jnp.sum(mixed * (hit1 - hit2), axis=-1, keepdims=True)
    high = gap.astype(BF16).astype(F32)
    mid = (gap - high).astype(BF16).astype(F32)
    rest = gap - high - mid
    extra = hit1 - hit2
    extra = jnp.where(lane == 16, high, extra)
    extra = jnp.where(lane == 17, mid, extra)
    extra = jnp.where(lane == 18, rest, extra)
    info[...] = mixed
    hits[:, :LANES] = hit1
    hits[:, LANES:] = hit2
    width = dy.shape[1]
    dy_send[:, :width] = dot_nn(table, dy[...]).astype(BF16)
    dy_send[:, width:] = dot_nn(signed, extra.astype(BF16)).astype(BF16)


def attend_jobs(par, job):
    half = (job >= 8).astype(jnp.int32)
    turn = job - 8
    shared = 2 * turn + ((turn + par) & 1)
    return jnp.where(half == 1, shared, job), half


def lane_pick(par, half, shape):
    lane = lax.broadcasted_iota(jnp.int32, shape, 1)
    low = lane < HDIM
    want = ((par + half) & 1) == 0
    return jnp.where(want, low.astype(F32), 1.0 - low.astype(F32))


def masked_scores(scores, label_q, label_k, tile, step):
    row = lax.broadcasted_iota(jnp.int32, scores.shape, 0) + step * KT
    col = lax.broadcasted_iota(jnp.int32, scores.shape, 1) + tile * QT
    seen = (row <= col) | (label_k == label_q)
    return jnp.where(seen, scores, NEGATIVE_FILL)


def fold_rows(values, op):
    return op(values.reshape(values.shape[0] // 8, 8, values.shape[1]), axis=0)


def attend_kernel(qkv, label_q, label_k, par_ref, low, context, lse, peaks, board, value_t):
    par = par_ref[0]
    length = qkv.shape[0]
    tiles = length // QT
    value_t[...] = qkv[:, 2 * LANES :].astype(F32).T.astype(BF16)
    context[...] = jnp.zeros_like(context)
    peaks[...] = jnp.full_like(peaks, NEGATIVE_FILL)
    lse[...] = jnp.zeros_like(lse)

    def run(job, carry):
        tile, half = attend_jobs(par, job)
        rows = pl.ds(pl.multiple_of(tile * QT, QT), QT)
        pick = lane_pick(par, half, (QT, LANES))
        query = (qkv[rows, :LANES].astype(F32) * (pick * 0.125)).astype(BF16)
        label = label_q[pl.ds(tile, 1), :]
        plain = tile // 2
        total = jnp.minimum((tile + 3) // 2, length // KT)

        def score(step, masked):
            span = pl.ds(pl.multiple_of(step * KT, KT), KT)
            scores = dot_nt(qkv[span, LANES : 2 * LANES], query)
            if masked:
                scores = masked_scores(scores, label, label_k[span, :], tile, step)
            board[span, :] = scores
            return fold_rows(scores, jnp.max)

        top = jnp.full((8, QT), NEGATIVE_FILL, F32)
        top = lax.fori_loop(0, plain, lambda j, c: jnp.maximum(c, score(j, False)), top)
        top = lax.fori_loop(plain, total, lambda j, c: jnp.maximum(c, score(j, True)), top)
        peak = jnp.max(top, axis=0, keepdims=True)

        def weigh(step, carry):
            sums, acc = carry
            span = pl.ds(pl.multiple_of(step * KT, KT), KT)
            power = jnp.exp(board[span, :] - peak)
            acc = acc + dot_nn(value_t[:, span], power.astype(BF16))
            return sums + fold_rows(power, jnp.sum), acc

        sums, acc = lax.fori_loop(
            0, total, weigh, (jnp.zeros((8, QT), F32), jnp.zeros((LANES, QT), F32))
        )
        norm = jnp.sum(sums, axis=0, keepdims=True)
        context[rows, :] += (acc / norm).T * pick
        slot = pl.ds(half * tiles + tile, 1)
        lse[slot, :] = peak + jnp.log(norm)
        peaks[slot, :] = peak
        return carry

    lax.fori_loop(0, 12, run, 0)
    low[...] = context[...].astype(BF16)


def attend_back_kernel(
    qkv, grad, context, lse, label_q, label_k, par_ref, out, dq, dk, dv, key_t
):
    par = par_ref[0]
    length = qkv.shape[0]
    tiles = length // QT
    key_t[...] = qkv[:, LANES : 2 * LANES].astype(F32).T.astype(BF16)
    dq[...] = jnp.zeros_like(dq)
    dk[...] = jnp.zeros_like(dk)
    dv[...] = jnp.zeros_like(dv)

    def run(job, carry):
        tile, half = attend_jobs(par, job)
        rows = pl.ds(pl.multiple_of(tile * QT, QT), QT)
        pick = lane_pick(par, half, (QT, LANES))
        query = (qkv[rows, :LANES].astype(F32) * (pick * 0.125)).astype(BF16)
        grad_wide = grad[rows, :].astype(F32) * pick
        grad_low = grad_wide.astype(BF16)
        delta = jnp.sum((grad_wide * context[rows, :]).T, axis=0, keepdims=True)
        label = label_q[pl.ds(tile, 1), :]
        bound = lse[pl.ds(half * tiles + tile, 1), :]
        plain = tile // 2
        total = jnp.minimum((tile + 3) // 2, length // KT)

        def step_of(step, acc, masked):
            span = pl.ds(pl.multiple_of(step * KT, KT), KT)
            scores = dot_nt(qkv[span, LANES : 2 * LANES], query)
            if masked:
                scores = masked_scores(scores, label, label_k[span, :], tile, step)
            power = jnp.exp(scores - bound)
            slope = dot_nt(qkv[span, 2 * LANES :], grad_low)
            score_grad = (power * (slope - delta)).astype(BF16)
            dv[span, :] += dot_nn(power.astype(BF16), grad_low)
            dk[span, :] += dot_nn(score_grad, query)
            return acc + dot_nn(key_t[:, span], score_grad)

        acc = jnp.zeros((LANES, QT), F32)
        acc = lax.fori_loop(0, plain, lambda j, c: step_of(j, c, False), acc)
        acc = lax.fori_loop(plain, total, lambda j, c: step_of(j, c, True), acc)
        dq[rows, :] += acc.T * (pick * 0.125)
        return carry

    lax.fori_loop(0, 12, run, 0)
    out[:, :LANES] = dq[...].astype(BF16)
    out[:, LANES : 2 * LANES] = dk[...].astype(BF16)
    out[:, 2 * LANES :] = dv[...].astype(BF16)


def middle_kernel(tokens, context, wo, gain, dispatch, middle, second_low, send):
    acc = tokens[...].astype(F32)
    for index in range(context.shape[0]):
        start = head_start(index)
        acc = acc + dot_nn(context[index], wo[start : start + LANES, :])
    middle[...] = acc
    scale = lax.rsqrt(jnp.mean(acc * acc, axis=-1, keepdims=True) + EPSILON)
    low = (acc * scale * gain[...]).astype(BF16)
    second_low[...] = low
    send[...] = dot_nn(dispatch[...], low).astype(BF16)


def side_kernel(
    second_low, dy_ref, hits, mixed, router, mixers, vectors, first_base, second_base, partial,
    gate, probs, smalls,
):
    low = second_low[...]
    norm = low.astype(F32)
    dy = dy_ref[...].astype(F32)
    rows = low.shape[0]
    lane = lax.broadcasted_iota(jnp.int32, (rows, LANES), 1)
    hit1 = hits[:, :LANES]
    hit2 = hits[:, LANES:]
    targets = EXPERTS + 2 + vectors.shape[0]
    logits = dot_nn(low, router[...]) + mixed[...]
    logits = jnp.where(lane < targets, logits, NEGATIVE_FILL)
    power = jnp.exp(logits - jnp.max(logits, axis=-1, keepdims=True))
    prob = power / jnp.sum(power, axis=-1, keepdims=True)
    probs[...] = prob
    pick1 = jnp.sum(prob * hit1, axis=-1, keepdims=True)
    pick2 = jnp.sum(prob * hit2, axis=-1, keepdims=True)
    total = pick1 + pick2
    share1 = pick1 / total
    share2 = pick2 / total
    gate[...] = jnp.where(lane == 0, share1, jnp.where(lane == 1, share2, total))
    mixer = dot_nt(low, mixers[...])
    copy = EXPERTS + 1
    base1 = hit1[:, copy : copy + 1] * norm
    base2 = hit2[:, copy : copy + 1] * norm
    back = (
        hit1[:, copy : copy + 1] * share1 + hit2[:, copy : copy + 1] * share2
    ) * dy
    smalls[...] = jnp.zeros_like(smalls)
    count = vectors.shape[0]
    for c in range(count):
        z0 = mixer[:, 2 * c : 2 * c + 1]
        z1 = mixer[:, 2 * c + 1 : 2 * c + 2]
        big = jnp.maximum(z0, z1)
        e0 = jnp.exp(z0 - big)
        e1 = jnp.exp(z1 - big)
        a0 = e0 / (e0 + e1)
        a1 = e1 / (e0 + e1)
        vector = vectors[c : c + 1, :]
        value = a0 * norm + a1 * vector
        col = copy + 1 + c
        p1 = hit1[:, col : col + 1]
        p2 = hit2[:, col : col + 1]
        base1 = base1 + p1 * value
        base2 = base2 + p2 * value
        grad = (p1 * share1 + p2 * share2) * dy
        back = back + a0 * grad
        smalls[c : c + 1, :] = jnp.sum(a1 * grad, axis=0, keepdims=True)
        g0 = jnp.sum(norm * grad, axis=-1, keepdims=True)
        g1 = jnp.sum(vector * grad, axis=-1, keepdims=True)
        inner = a0 * g0 + a1 * g1
        d0 = a0 * (g0 - inner)
        d1 = a1 * (g1 - inner)
        back = back + d0 * mixers[2 * c : 2 * c + 1, :].astype(F32)
        back = back + d1 * mixers[2 * c + 1 : 2 * c + 2, :].astype(F32)
        smalls[count + 2 * c : count + 2 * c + 1, :] = jnp.sum(d0 * norm, axis=0, keepdims=True)
        smalls[count + 2 * c + 1 : count + 2 * c + 2, :] = jnp.sum(
            d1 * norm, axis=0, keepdims=True
        )
    first_base[...] = base1
    second_base[...] = base2
    partial[...] = back


def output_kernel(
    returned, first_t, second_t, middle, first_base, second_base, dy_ref, gate, probs, hits,
    second_low, router, prev, mix, partial, output, back, prev_grad, router_grad, mix_grad,
):
    got = returned[...]
    branch1 = dot_nn(first_t[...], got) + first_base[...]
    branch2 = dot_nn(second_t[...], got) + second_base[...]
    share1 = gate[:, 0:1]
    share2 = gate[:, 1:2]
    total = gate[:, 2:3]
    output[...] = (middle[...] + share1 * branch1 + share2 * branch2).astype(BF16)
    dy = dy_ref[...].astype(F32)
    d1 = jnp.sum(branch1 * dy, axis=-1, keepdims=True)
    d2 = jnp.sum(branch2 * dy, axis=-1, keepdims=True)
    inner = share1 * d1 + share2 * d2
    prob_grad = hits[:, :LANES] * ((d1 - inner) / total) + hits[:, LANES:] * (
        (d2 - inner) / total
    )
    prob = probs[...]
    logit_grad = prob * (prob_grad - jnp.sum(prob * prob_grad, axis=-1, keepdims=True))
    back[...] = partial[...] + dot_nt(logit_grad, router[...].astype(F32), HIGHEST)
    prev_grad[...] = dot_nt(logit_grad, mix[...], HIGHEST)
    turned = logit_grad.T
    router_grad[...] = dot_nn(turned, second_low[...].astype(F32), HIGHEST)[:16]
    mix_grad[...] = dot_nn(turned, prev[...], HIGHEST)[:16]


def middle_back_kernel(
    returned, first_t, second_t, partial, middle, gain, dy_ref, wo, grad, grad_low, send, gain_grad
):
    table = first_t[...] + second_t[...]
    second = partial[...] + dot_nn(table, returned[...])
    mid = middle[...]
    scale = lax.rsqrt(jnp.mean(mid * mid, axis=-1, keepdims=True) + EPSILON)
    scaled = second * gain[...]
    inner = jnp.mean(scaled * mid, axis=-1, keepdims=True)
    out = dy_ref[...].astype(F32) + scale * (scaled - mid * (scale * scale * inner))
    gain_grad[...] = jnp.sum(second * mid * scale, axis=0, keepdims=True)
    grad[...] = out
    low = out.astype(BF16)
    grad_low[...] = low
    for index in range(send.shape[0]):
        start = head_start(index)
        send[index] = dot_nt(low, wo[start : start + LANES, :]).astype(BF16)


def input_kernel(returned, wq, wk, wv, tokens, gain, middle_grad, grad, gain_grad):
    acc = jnp.zeros(middle_grad.shape, F32)
    for part, weight in enumerate((wq, wk, wv)):
        full = weight[...]
        for index in range(returned.shape[0]):
            start = head_start(index)
            acc = acc + dot_nt(
                returned[index, :, part * LANES : (part + 1) * LANES],
                full[:, start : start + LANES],
            )
    x = tokens[...].astype(F32)
    scale = lax.rsqrt(jnp.mean(x * x, axis=-1, keepdims=True) + EPSILON)
    scaled = acc * gain[...]
    inner = jnp.mean(scaled * x, axis=-1, keepdims=True)
    grad[...] = middle_grad[...] + scale * (scaled - x * (scale * scale * inner))
    gain_grad[...] = jnp.sum(acc * x * scale, axis=0, keepdims=True)


def join_heads(parts, axis):
    pieces = []
    for pair in range(parts.shape[0] // 2):
        a, b = parts[2 * pair], parts[2 * pair + 1]
        a0, a1 = jnp.split(a, 2, axis=axis)
        b0, b1 = jnp.split(b, 2, axis=axis)
        pieces += [a0, a1 + b0, b1]
    return jnp.concatenate(pieces, axis=axis)


def body(
    tokens,
    routes,
    pieces,
    prev_logits,
    cotangent,
    first_gain,
    query_weight,
    key_weight,
    value_weight,
    out_weight,
    second_gain,
    router_weight,
    gate_mix,
    const_mixer,
    const_vector,
    expert_gate,
    expert_up,
    expert_down,
):
    seq_count, seq_dev, width = tokens.shape
    group = lax.axis_size("expert")
    replicas = lax.axis_size("dp")
    devices = group * replicas
    length = seq_dev * group
    targets = router_weight.shape[1]
    most = seq_dev // 4
    slots = EXPERTS * most
    both = ("dp", "expert")
    assert seq_count == 1 and HEADS * 2 == 3 * group and expert_gate.shape[0] == 1

    rows = tokens.reshape(seq_dev, width)
    dy = cotangent.reshape(seq_dev, width)
    parity = (lax.axis_index("expert") % 2).astype(jnp.int32).reshape(1)
    gain1 = first_gain.reshape(1, width)
    gain2 = second_gain.reshape(1, width)
    prev_pad = jnp.pad(prev_logits.reshape(seq_dev, targets), ((0, 0), (0, LANES - targets)))
    mix_pad = jnp.pad(gate_mix, ((0, LANES - targets), (0, LANES - targets)))
    router_pad = jnp.pad(router_weight, ((0, 0), (0, LANES - targets)))
    count = const_vector.shape[0]
    mixers_pad = jnp.pad(const_mixer.reshape(2 * count, width), ((0, LANES - 2 * count), (0, 0)))

    def exchange(values, axes):
        return lax.all_to_all(values, axes, split_axis=0, concat_axis=0, tiled=True)

    first_low, qkv_send = call(
        project_kernel,
        (struct((seq_dev, width), BF16), struct((group, seq_dev, 3 * LANES), BF16)),
        rows, gain1, query_weight, key_weight, value_weight,
        flops=2 * seq_dev * width * width * 3,
    )
    qkv = exchange(qkv_send, "expert").reshape(length, 3 * LANES)
    first_all = lax.all_gather(first_low, "expert", axis=0, tiled=True)

    dispatch, first_t, second_t, mixed, hits, dy_send = call(
        route_kernel,
        (
            struct((slots, seq_dev), BF16),
            struct((seq_dev, slots), BF16),
            struct((seq_dev, slots), BF16),
            struct((seq_dev, LANES), F32),
            struct((seq_dev, 2 * LANES), F32),
            struct((slots, width + LANES), BF16),
        ),
        routes.reshape(seq_dev, 2), prev_pad, mix_pad, dy,
        flops=2 * slots * seq_dev * width,
    )
    arrived = exchange(
        dy_send.reshape(group, most, width + LANES), "expert"
    ).reshape(slots, width + LANES)
    dy_rows = arrived[:, :width]
    info = arrived[:, width:].astype(F32)
    down = expert_down[0]
    hidden_back = dot_nt(dy_rows, down)

    positions = jnp.arange(length, dtype=jnp.int32)
    starts = pieces.reshape(-1)
    inside = (positions[:, None] >= starts[None, :]) & (
        positions[:, None] < starts[None, :] + PIECE
    )
    numbers = jnp.arange(1, starts.shape[0] + 1, dtype=jnp.int32)
    labels = jnp.sum(jnp.where(inside, numbers[None, :], 0), axis=1)
    label_q = jnp.where(labels == 0, -1, labels).reshape(length // QT, QT)
    label_k = labels.reshape(length, 1)
    tiles = length // QT
    attend_flops = 54 * QT * QT * LANES * 2
    context_low, context, lse, peaks = call(
        attend_kernel,
        (
            struct((length, LANES), BF16),
            struct((length, LANES), F32),
            struct((2 * tiles, QT), F32),
            struct((2 * tiles, QT), F32),
        ),
        qkv, label_q, label_k, parity,
        scratch=(pltpu.VMEM((length, QT), F32), pltpu.VMEM((LANES, length), BF16)),
        smem=(3,),
        flops=2 * attend_flops,
    )
    heads = exchange(context_low.reshape(group, seq_dev, LANES), "expert")

    middle, second_low, row_send = call(
        middle_kernel,
        (
            struct((seq_dev, width), F32),
            struct((seq_dev, width), BF16),
            struct((slots, width), BF16),
        ),
        rows, heads, out_weight, gain2, dispatch,
        flops=2 * seq_dev * width * 1024 + 2 * slots * seq_dev * width,
    )
    x = exchange(row_send.reshape(group, most, width), "expert").reshape(slots, width)
    first_base, second_base, partial, gate, probs, smalls = call(
        side_kernel,
        (
            struct((seq_dev, width), F32),
            struct((seq_dev, width), F32),
            struct((seq_dev, width), F32),
            struct((seq_dev, LANES), F32),
            struct((seq_dev, LANES), F32),
            struct((8, width), F32),
        ),
        second_low, dy, hits, mixed, router_pad, mixers_pad, const_vector,
        flops=4 * seq_dev * width * LANES,
    )

    wide_gate, wide_up = expert_gate[0], expert_up[0]
    gate_act = dot_nn(x, wide_gate)
    up_act = dot_nn(x, wide_up)
    sigmoid = jax.nn.sigmoid(gate_act)
    silu = gate_act * sigmoid
    hidden = (silu * up_act).astype(BF16)
    result = dot_nn(hidden, down).astype(BF16)
    returned = exchange(result.reshape(group, most, width), "expert").reshape(slots, width)
    gap = jnp.sum(dot_nn(x, router_weight) * info[:, :targets], axis=-1, keepdims=True)
    gap = gap + jnp.sum(info[:, 16:19], axis=-1, keepdims=True)
    share = jax.nn.sigmoid(gap)
    dy_route = (share * dy_rows.astype(F32)).astype(BF16)
    hidden_grad = share * hidden_back
    gate_low = (
        hidden_grad * up_act * sigmoid * (1.0 + gate_act * (1.0 - sigmoid))
    ).astype(BF16)
    up_low = (hidden_grad * silu).astype(BF16)
    x_grad = (dot_nt(gate_low, wide_gate) + dot_nt(up_low, wide_up)).astype(BF16)
    x_back = exchange(x_grad.reshape(group, most, width), "expert").reshape(slots, width)
    gate_local = dot_tn(x, gate_low).astype(BF16)
    up_local = dot_tn(x, up_low).astype(BF16)
    down_local = dot_tn(hidden, dy_route).astype(BF16)
    expert_parts = [
        lax.psum_scatter(v, "dp", scatter_dimension=0, tiled=True).astype(F32)[None]
        for v in (gate_local, up_local, down_local)
    ]

    output, back, prev_grad, router_local, mix_local = call(
        output_kernel,
        (
            struct((seq_dev, width), BF16),
            struct((seq_dev, width), F32),
            struct((seq_dev, LANES), F32),
            struct((16, width), F32),
            struct((16, LANES), F32),
        ),
        returned, first_t, second_t, middle, first_base, second_base, dy, gate, probs, hits,
        second_low, router_pad, prev_pad, mix_pad, partial,
        flops=4 * slots * seq_dev * width,
    )
    middle_grad, branch_low, grad_send, gain2_local = call(
        middle_back_kernel,
        (
            struct((seq_dev, width), F32),
            struct((seq_dev, width), BF16),
            struct((group, seq_dev, LANES), BF16),
            struct((1, width), F32),
        ),
        x_back, first_t, second_t, back, middle, gain2, dy, out_weight,
        flops=2 * slots * seq_dev * width + 2 * seq_dev * width * 1024,
    )
    context_grad = exchange(grad_send, "expert").reshape(length, LANES)

    out_local = join_heads(
        lax.dot_general(
            heads, branch_low, (((1,), (0,)), ((), ())), preferred_element_type=F32
        ),
        0,
    )
    out_grad = jnp.sum(
        exchange(out_local.astype(BF16).reshape(devices, -1, width), both)
        .astype(F32)
        .reshape(devices, -1, width),
        axis=0,
    )
    own = width // devices
    tops = jnp.stack([jnp.max(peaks[:tiles]), jnp.max(peaks[tiles:])])
    columns = jnp.concatenate([gain2_local, router_local[:targets], smalls[: 3 * count]], axis=0)
    kinds = columns.shape[0]
    columns = columns.reshape(kinds, devices, own).transpose(1, 0, 2).reshape(devices, -1)
    shared = jnp.concatenate([mix_local[:targets, :targets].T.reshape(-1), tops])
    packed = jnp.concatenate(
        [columns, jnp.broadcast_to(shared[None], (devices, shared.size))], axis=1
    )
    size = packed.shape[1]
    packed = jnp.pad(packed, ((0, 0), (0, -size % LANES)))
    gathered = exchange(packed.reshape(devices, -1, LANES), both).reshape(devices, -1)
    summed = jnp.sum(gathered[:, : kinds * own], axis=0).reshape(kinds, own)
    mix_grad = jnp.sum(
        gathered[:, kinds * own : kinds * own + targets * targets], axis=0
    ).reshape(targets, targets)
    tops = jnp.max(gathered[:, size - 2 : size].reshape(replicas, group, 2), axis=0)
    pairs = tops.reshape(group // 2, 2, 2)
    head_top = jnp.stack(
        [pairs[:, 0, 0], jnp.maximum(pairs[:, 0, 1], pairs[:, 1, 1]), pairs[:, 1, 0]], axis=1
    ).reshape(HEADS)
    factors = jnp.minimum(1.0, CLIP_LIMIT / head_top)
    root = jnp.repeat(jnp.sqrt(factors), HDIM)
    clipped_query = (query_weight.astype(F32) * root[None, :]).astype(BF16)
    clipped_key = (key_weight.astype(F32) * root[None, :]).astype(BF16)

    qkv_grad = call(
        attend_back_kernel,
        struct((length, 3 * LANES), BF16),
        qkv, context_grad, context, lse, label_q, label_k, parity,
        scratch=(
            pltpu.VMEM((length, LANES), F32),
            pltpu.VMEM((length, LANES), F32),
            pltpu.VMEM((length, LANES), F32),
            pltpu.VMEM((LANES, length), BF16),
        ),
        smem=(6,),
        flops=5 * attend_flops,
    )
    home = exchange(qkv_grad.reshape(group, seq_dev, 3 * LANES), "expert")
    weight_local = dot_tn(first_all, qkv_grad).astype(BF16)
    weight_parts = exchange(weight_local.reshape(devices, own, 3 * LANES), both)
    weight_sum = jnp.sum(
        weight_parts.astype(F32).reshape(replicas, group, own, 3 * LANES), axis=0
    )
    query_grad, key_grad, value_grad = [
        join_heads(weight_sum[:, :, part * LANES : (part + 1) * LANES], 1) for part in range(3)
    ]
    input_grad, gain1_local = call(
        input_kernel,
        (struct((seq_dev, width), F32), struct((1, width), F32)),
        home, query_weight, key_weight, value_weight, rows, gain1, middle_grad,
        flops=2 * seq_dev * width * 3072,
    )
    gain1_grad = jnp.sum(
        exchange(gain1_local.reshape(devices, 1, own), both).reshape(devices, own), axis=0
    )
    return (
        output.reshape(tokens.shape),
        input_grad.reshape(tokens.shape),
        prev_grad[:, :targets].reshape(prev_logits.shape),
        gain1_grad,
        query_grad,
        key_grad,
        value_grad,
        out_grad,
        summed[0],
        summed[1 : 1 + targets].T,
        mix_grad,
        summed[1 + targets + count : 1 + targets + 3 * count].reshape(count, 2, own),
        summed[1 + targets : 1 + targets + count],
        expert_parts[0],
        expert_parts[1],
        expert_parts[2],
        clipped_query,
        clipped_key,
        factors,
    )


def solution(mesh):
    tokens = P("dp", "expert", None)
    experts = P("expert", None, None)
    dense = P(("dp", "expert"), None)
    parts = P("expert", "dp", None)
    return jax.shard_map(
        body,
        mesh=mesh,
        in_specs=(tokens, tokens, P("dp", None), tokens, tokens)
        + (P(),) * 10
        + (experts, experts, experts),
        out_specs=(
            tokens,
            tokens,
            tokens,
            P(("dp", "expert")),
            dense,
            dense,
            dense,
            dense,
            P(("dp", "expert")),
            dense,
            P(),
            P(None, None, ("dp", "expert")),
            P(None, ("dp", "expert")),
            parts,
            parts,
            parts,
            P(),
            P(),
            P(),
        ),
        check_vma=False,
    )
```

```python
import functools

import jax
import jax.numpy as jnp
from jax import lax
from jax.experimental import pallas as pl
from jax.experimental.pallas import tpu as pltpu
from jax.sharding import PartitionSpec as P

HEADS = 12
HDIM = 64
EXPERTS = 8
PIECE = 256
EPSILON = 1e-06
CLIP_LIMIT = 2.0
NEGATIVE_FILL = -1e30
HIGHEST = lax.Precision.HIGHEST
LANES = 128
F32 = jnp.float32
BF16 = jnp.bfloat16
VMEM_BYTES = 60 * 1024 * 1024
QT = 256
KT = 512


def dot_nn(a, b, precision=None):
    return lax.dot_general(
        a, b, (((1,), (0,)), ((), ())), preferred_element_type=F32, precision=precision
    )


def dot_nt(a, b, precision=None):
    return lax.dot_general(
        a, b, (((1,), (1,)), ((), ())), preferred_element_type=F32, precision=precision
    )


def dot_tn(a, b, precision=None):
    return lax.dot_general(
        a, b, (((0,), (0,)), ((), ())), preferred_element_type=F32, precision=precision
    )


def head_start(index):
    return (index // 2) * 3 * HDIM + (index % 2) * HDIM


def call(body, out_shape, *args, scratch=(), smem=(), flops=0):
    vmem = pl.BlockSpec(memory_space=pltpu.VMEM)
    specs = [
        pl.BlockSpec(memory_space=pltpu.SMEM) if i in smem else vmem for i in range(len(args))
    ]
    outs = jax.tree.leaves(out_shape)
    nbytes = sum(a.size * a.dtype.itemsize for a in list(args) + outs)
    return pl.pallas_call(
        body,
        out_shape=out_shape,
        in_specs=specs,
        out_specs=jax.tree.map(lambda _: vmem, out_shape),
        scratch_shapes=list(scratch),
        compiler_params=pltpu.CompilerParams(vmem_limit_bytes=VMEM_BYTES),
        cost_estimate=pl.CostEstimate(flops=flops, bytes_accessed=nbytes, transcendentals=0),
    )(*args)


def struct(shape, dtype):
    return jax.ShapeDtypeStruct(shape, dtype)


def project_kernel(tokens, gain, wq, wk, wv, first_low, send):
    x = tokens[...].astype(F32)
    scale = lax.rsqrt(jnp.mean(x * x, axis=-1, keepdims=True) + EPSILON)
    low = (x * scale * gain[...]).astype(BF16)
    first_low[...] = low
    for part, weight in enumerate((wq, wk, wv)):
        full = dot_nn(low, weight[...])
        for index in range(send.shape[0]):
            start = head_start(index)
            send[index, :, part * LANES : (part + 1) * LANES] = full[
                :, start : start + LANES
            ].astype(BF16)


def route_kernel(routes, prev, mix, dy, dispatch, first_t, second_t, info, hits, dy_send):
    rows = routes.shape[0]
    slots = dispatch.shape[0]
    most = slots // EXPERTS
    lane = lax.broadcasted_iota(jnp.int32, (rows, LANES), 1)
    ids = routes[...]
    hit1 = (ids[:, 0:1] == lane).astype(F32)
    hit2 = (ids[:, 1:2] == lane).astype(F32)
    before = (
        lax.broadcasted_iota(jnp.int32, (rows, rows), 1)
        < lax.broadcasted_iota(jnp.int32, (rows, rows), 0)
    ).astype(F32)
    rank = dot_nn(before.astype(BF16), (hit1 + hit2).astype(BF16))
    spread = (
        lax.broadcasted_iota(jnp.int32, (LANES, slots), 0)
        == lax.broadcasted_iota(jnp.int32, (LANES, slots), 1) // most
    ).astype(F32).astype(BF16)
    place = (lax.broadcasted_iota(jnp.int32, (rows, slots), 1) % most).astype(F32)
    here = (dot_nn(rank.astype(BF16), spread) == place).astype(F32)
    one = here * dot_nn(hit1.astype(BF16), spread)
    two = here * dot_nn(hit2.astype(BF16), spread)
    first_t[...] = one.astype(BF16)
    second_t[...] = two.astype(BF16)
    table = (one + two).T.astype(BF16)
    signed = (one - two).T.astype(BF16)
    dispatch[...] = table
    mixed = dot_nn(prev[...], mix[...], HIGHEST)
    gap = jnp.sum(mixed * (hit1 - hit2), axis=-1, keepdims=True)
    high = gap.astype(BF16).astype(F32)
    mid = (gap - high).astype(BF16).astype(F32)
    rest = gap - high - mid
    extra = hit1 - hit2
    extra = jnp.where(lane == 16, high, extra)
    extra = jnp.where(lane == 17, mid, extra)
    extra = jnp.where(lane == 18, rest, extra)
    info[...] = mixed
    hits[:, :LANES] = hit1
    hits[:, LANES:] = hit2
    width = dy.shape[1]
    dy_send[:, :width] = dot_nn(table, dy[...]).astype(BF16)
    dy_send[:, width:] = dot_nn(signed, extra.astype(BF16)).astype(BF16)


def attend_jobs(par, job):
    half = (job >= 8).astype(jnp.int32)
    turn = job - 8
    shared = 2 * turn + ((turn + par) & 1)
    return jnp.where(half == 1, shared, job), half


def lane_pick(par, half, shape):
    lane = lax.broadcasted_iota(jnp.int32, shape, 1)
    low = lane < HDIM
    want = ((par + half) & 1) == 0
    return jnp.where(want, low.astype(F32), 1.0 - low.astype(F32))


def masked_scores(scores, label_q, label_k, tile, step):
    row = lax.broadcasted_iota(jnp.int32, scores.shape, 0) + step * KT
    col = lax.broadcasted_iota(jnp.int32, scores.shape, 1) + tile * QT
    seen = (row <= col) | (label_k == label_q)
    return jnp.where(seen, scores, NEGATIVE_FILL)


def fold_rows(values, op):
    return op(values.reshape(values.shape[0] // 8, 8, values.shape[1]), axis=0)


def attend_kernel(qkv, label_q, label_k, par_ref, low, context, lse, peaks, board, value_t):
    par = par_ref[0]
    length = qkv.shape[0]
    tiles = length // QT
    value_t[...] = qkv[:, 2 * LANES :].astype(F32).T.astype(BF16)
    context[...] = jnp.zeros_like(context)
    peaks[...] = jnp.full_like(peaks, NEGATIVE_FILL)
    lse[...] = jnp.zeros_like(lse)

    def run(job, carry):
        tile, half = attend_jobs(par, job)
        rows = pl.ds(pl.multiple_of(tile * QT, QT), QT)
        pick = lane_pick(par, half, (QT, LANES))
        query = (qkv[rows, :LANES].astype(F32) * (pick * 0.125)).astype(BF16)
        label = label_q[pl.ds(tile, 1), :]
        plain = tile // 2
        total = jnp.minimum((tile + 3) // 2, length // KT)

        def score(step, masked):
            span = pl.ds(pl.multiple_of(step * KT, KT), KT)
            scores = dot_nt(qkv[span, LANES : 2 * LANES], query)
            if masked:
                scores = masked_scores(scores, label, label_k[span, :], tile, step)
            board[span, :] = scores
            return fold_rows(scores, jnp.max)

        top = jnp.full((8, QT), NEGATIVE_FILL, F32)
        top = lax.fori_loop(0, plain, lambda j, c: jnp.maximum(c, score(j, False)), top)
        top = lax.fori_loop(plain, total, lambda j, c: jnp.maximum(c, score(j, True)), top)
        peak = jnp.max(top, axis=0, keepdims=True)

        def weigh(step, carry):
            sums, acc = carry
            span = pl.ds(pl.multiple_of(step * KT, KT), KT)
            power = jnp.exp(board[span, :] - peak)
            acc = acc + dot_nn(value_t[:, span], power.astype(BF16))
            return sums + fold_rows(power, jnp.sum), acc

        sums, acc = lax.fori_loop(
            0, total, weigh, (jnp.zeros((8, QT), F32), jnp.zeros((LANES, QT), F32))
        )
        norm = jnp.sum(sums, axis=0, keepdims=True)
        context[rows, :] += (acc / norm).T * pick
        slot = pl.ds(half * tiles + tile, 1)
        lse[slot, :] = peak + jnp.log(norm)
        peaks[slot, :] = peak
        return carry

    lax.fori_loop(0, 12, run, 0)
    low[...] = context[...].astype(BF16)


def attend_back_kernel(
    qkv, grad, context, lse, label_q, label_k, par_ref, out, dq, dk, dv, key_t
):
    par = par_ref[0]
    length = qkv.shape[0]
    tiles = length // QT
    key_t[...] = qkv[:, LANES : 2 * LANES].astype(F32).T.astype(BF16)
    dq[...] = jnp.zeros_like(dq)
    dk[...] = jnp.zeros_like(dk)
    dv[...] = jnp.zeros_like(dv)

    def run(job, carry):
        tile, half = attend_jobs(par, job)
        rows = pl.ds(pl.multiple_of(tile * QT, QT), QT)
        pick = lane_pick(par, half, (QT, LANES))
        query = (qkv[rows, :LANES].astype(F32) * (pick * 0.125)).astype(BF16)
        grad_wide = grad[rows, :].astype(F32) * pick
        grad_low = grad_wide.astype(BF16)
        delta = jnp.sum((grad_wide * context[rows, :]).T, axis=0, keepdims=True)
        label = label_q[pl.ds(tile, 1), :]
        bound = lse[pl.ds(half * tiles + tile, 1), :]
        plain = tile // 2
        total = jnp.minimum((tile + 3) // 2, length // KT)

        def step_of(step, acc, masked):
            span = pl.ds(pl.multiple_of(step * KT, KT), KT)
            scores = dot_nt(qkv[span, LANES : 2 * LANES], query)
            if masked:
                scores = masked_scores(scores, label, label_k[span, :], tile, step)
            power = jnp.exp(scores - bound)
            slope = dot_nt(qkv[span, 2 * LANES :], grad_low)
            score_grad = (power * (slope - delta)).astype(BF16)
            dv[span, :] += dot_nn(power.astype(BF16), grad_low)
            dk[span, :] += dot_nn(score_grad, query)
            return acc + dot_nn(key_t[:, span], score_grad)

        acc = jnp.zeros((LANES, QT), F32)
        acc = lax.fori_loop(0, plain, lambda j, c: step_of(j, c, False), acc)
        acc = lax.fori_loop(plain, total, lambda j, c: step_of(j, c, True), acc)
        dq[rows, :] += acc.T * (pick * 0.125)
        return carry

    lax.fori_loop(0, 12, run, 0)
    out[:, :LANES] = dq[...].astype(BF16)
    out[:, LANES : 2 * LANES] = dk[...].astype(BF16)
    out[:, 2 * LANES :] = dv[...].astype(BF16)


def middle_kernel(tokens, context, wo, gain, dispatch, middle, second_low, send):
    acc = tokens[...].astype(F32)
    for index in range(context.shape[0]):
        start = head_start(index)
        acc = acc + dot_nn(context[index], wo[start : start + LANES, :])
    middle[...] = acc
    scale = lax.rsqrt(jnp.mean(acc * acc, axis=-1, keepdims=True) + EPSILON)
    low = (acc * scale * gain[...]).astype(BF16)
    second_low[...] = low
    send[...] = dot_nn(dispatch[...], low).astype(BF16)


def side_kernel(
    second_low, dy_ref, hits, mixed, router, mixers, vectors, first_base, second_base, partial,
    gate, probs, smalls,
):
    low = second_low[...]
    norm = low.astype(F32)
    dy = dy_ref[...].astype(F32)
    rows = low.shape[0]
    lane = lax.broadcasted_iota(jnp.int32, (rows, LANES), 1)
    hit1 = hits[:, :LANES]
    hit2 = hits[:, LANES:]
    targets = EXPERTS + 2 + vectors.shape[0]
    logits = dot_nn(low, router[...]) + mixed[...]
    logits = jnp.where(lane < targets, logits, NEGATIVE_FILL)
    power = jnp.exp(logits - jnp.max(logits, axis=-1, keepdims=True))
    prob = power / jnp.sum(power, axis=-1, keepdims=True)
    probs[...] = prob
    pick1 = jnp.sum(prob * hit1, axis=-1, keepdims=True)
    pick2 = jnp.sum(prob * hit2, axis=-1, keepdims=True)
    total = pick1 + pick2
    share1 = pick1 / total
    share2 = pick2 / total
    gate[...] = jnp.where(lane == 0, share1, jnp.where(lane == 1, share2, total))
    mixer = dot_nt(low, mixers[...])
    copy = EXPERTS + 1
    base1 = hit1[:, copy : copy + 1] * norm
    base2 = hit2[:, copy : copy + 1] * norm
    back = (
        hit1[:, copy : copy + 1] * share1 + hit2[:, copy : copy + 1] * share2
    ) * dy
    smalls[...] = jnp.zeros_like(smalls)
    count = vectors.shape[0]
    for c in range(count):
        z0 = mixer[:, 2 * c : 2 * c + 1]
        z1 = mixer[:, 2 * c + 1 : 2 * c + 2]
        big = jnp.maximum(z0, z1)
        e0 = jnp.exp(z0 - big)
        e1 = jnp.exp(z1 - big)
        a0 = e0 / (e0 + e1)
        a1 = e1 / (e0 + e1)
        vector = vectors[c : c + 1, :]
        value = a0 * norm + a1 * vector
        col = copy + 1 + c
        p1 = hit1[:, col : col + 1]
        p2 = hit2[:, col : col + 1]
        base1 = base1 + p1 * value
        base2 = base2 + p2 * value
        grad = (p1 * share1 + p2 * share2) * dy
        back = back + a0 * grad
        smalls[c : c + 1, :] = jnp.sum(a1 * grad, axis=0, keepdims=True)
        g0 = jnp.sum(norm * grad, axis=-1, keepdims=True)
        g1 = jnp.sum(vector * grad, axis=-1, keepdims=True)
        inner = a0 * g0 + a1 * g1
        d0 = a0 * (g0 - inner)
        d1 = a1 * (g1 - inner)
        back = back + d0 * mixers[2 * c : 2 * c + 1, :].astype(F32)
        back = back + d1 * mixers[2 * c + 1 : 2 * c + 2, :].astype(F32)
        smalls[count + 2 * c : count + 2 * c + 1, :] = jnp.sum(d0 * norm, axis=0, keepdims=True)
        smalls[count + 2 * c + 1 : count + 2 * c + 2, :] = jnp.sum(
            d1 * norm, axis=0, keepdims=True
        )
    first_base[...] = base1
    second_base[...] = base2
    partial[...] = back


def output_kernel(
    returned, first_t, second_t, middle, first_base, second_base, dy_ref, gate, probs, hits,
    second_low, router, prev, mix, partial, output, back, prev_grad, router_grad, mix_grad,
):
    got = returned[...]
    branch1 = dot_nn(first_t[...], got) + first_base[...]
    branch2 = dot_nn(second_t[...], got) + second_base[...]
    share1 = gate[:, 0:1]
    share2 = gate[:, 1:2]
    total = gate[:, 2:3]
    output[...] = (middle[...] + share1 * branch1 + share2 * branch2).astype(BF16)
    dy = dy_ref[...].astype(F32)
    d1 = jnp.sum(branch1 * dy, axis=-1, keepdims=True)
    d2 = jnp.sum(branch2 * dy, axis=-1, keepdims=True)
    inner = share1 * d1 + share2 * d2
    prob_grad = hits[:, :LANES] * ((d1 - inner) / total) + hits[:, LANES:] * (
        (d2 - inner) / total
    )
    prob = probs[...]
    logit_grad = prob * (prob_grad - jnp.sum(prob * prob_grad, axis=-1, keepdims=True))
    back[...] = partial[...] + dot_nt(logit_grad, router[...].astype(F32), HIGHEST)
    prev_grad[...] = dot_nt(logit_grad, mix[...], HIGHEST)
    turned = logit_grad.T
    router_grad[...] = dot_nn(turned, second_low[...].astype(F32), HIGHEST)[:16]
    mix_grad[...] = dot_nn(turned, prev[...], HIGHEST)[:16]


def middle_back_kernel(
    returned, first_t, second_t, partial, middle, gain, dy_ref, wo, grad, grad_low, send, gain_grad
):
    table = first_t[...] + second_t[...]
    second = partial[...] + dot_nn(table, returned[...])
    mid = middle[...]
    scale = lax.rsqrt(jnp.mean(mid * mid, axis=-1, keepdims=True) + EPSILON)
    scaled = second * gain[...]
    inner = jnp.mean(scaled * mid, axis=-1, keepdims=True)
    out = dy_ref[...].astype(F32) + scale * (scaled - mid * (scale * scale * inner))
    gain_grad[...] = jnp.sum(second * mid * scale, axis=0, keepdims=True)
    grad[...] = out
    low = out.astype(BF16)
    grad_low[...] = low
    for index in range(send.shape[0]):
        start = head_start(index)
        send[index] = dot_nt(low, wo[start : start + LANES, :]).astype(BF16)


def input_kernel(returned, wq, wk, wv, tokens, gain, middle_grad, grad, gain_grad):
    acc = jnp.zeros(middle_grad.shape, F32)
    for part, weight in enumerate((wq, wk, wv)):
        full = weight[...]
        for index in range(returned.shape[0]):
            start = head_start(index)
            acc = acc + dot_nt(
                returned[index, :, part * LANES : (part + 1) * LANES],
                full[:, start : start + LANES],
            )
    x = tokens[...].astype(F32)
    scale = lax.rsqrt(jnp.mean(x * x, axis=-1, keepdims=True) + EPSILON)
    scaled = acc * gain[...]
    inner = jnp.mean(scaled * x, axis=-1, keepdims=True)
    grad[...] = middle_grad[...] + scale * (scaled - x * (scale * scale * inner))
    gain_grad[...] = jnp.sum(acc * x * scale, axis=0, keepdims=True)


def join_heads(parts, axis):
    pieces = []
    for pair in range(parts.shape[0] // 2):
        a, b = parts[2 * pair], parts[2 * pair + 1]
        a0, a1 = jnp.split(a, 2, axis=axis)
        b0, b1 = jnp.split(b, 2, axis=axis)
        pieces += [a0, a1 + b0, b1]
    return jnp.concatenate(pieces, axis=axis)


def body(
    tokens,
    routes,
    pieces,
    prev_logits,
    cotangent,
    first_gain,
    query_weight,
    key_weight,
    value_weight,
    out_weight,
    second_gain,
    router_weight,
    gate_mix,
    const_mixer,
    const_vector,
    expert_gate,
    expert_up,
    expert_down,
):
    seq_count, seq_dev, width = tokens.shape
    group = lax.axis_size("expert")
    replicas = lax.axis_size("dp")
    devices = group * replicas
    length = seq_dev * group
    targets = router_weight.shape[1]
    most = seq_dev // 4
    slots = EXPERTS * most
    both = ("dp", "expert")
    assert seq_count == 1 and HEADS * 2 == 3 * group and expert_gate.shape[0] == 1

    rows = tokens.reshape(seq_dev, width)
    dy = cotangent.reshape(seq_dev, width)
    parity = (lax.axis_index("expert") % 2).astype(jnp.int32).reshape(1)
    gain1 = first_gain.reshape(1, width)
    gain2 = second_gain.reshape(1, width)
    prev_pad = jnp.pad(prev_logits.reshape(seq_dev, targets), ((0, 0), (0, LANES - targets)))
    mix_pad = jnp.pad(gate_mix, ((0, LANES - targets), (0, LANES - targets)))
    router_pad = jnp.pad(router_weight, ((0, 0), (0, LANES - targets)))
    count = const_vector.shape[0]
    mixers_pad = jnp.pad(const_mixer.reshape(2 * count, width), ((0, LANES - 2 * count), (0, 0)))

    def exchange(values, axes):
        return lax.all_to_all(values, axes, split_axis=0, concat_axis=0, tiled=True)

    tie = lax.optimization_barrier

    def butterfly(values):
        bits = replicas.bit_length() - 1
        assert replicas == 1 << bits
        index = lax.axis_index("dp")
        shape = values.shape
        values = values.reshape((2,) * bits + (-1,) + shape[1:])
        for bit in range(bits):
            axis = bits - 1 - bit
            mine = (index >> bit) & 1
            kept = lax.dynamic_index_in_dim(values, mine, axis, keepdims=False)
            sent = lax.dynamic_index_in_dim(values, 1 - mine, axis, keepdims=False)
            ring = [(i, i ^ (1 << bit)) for i in range(replicas)]
            values = kept + lax.ppermute(sent.astype(BF16), "dp", ring).astype(F32)
        return values

    first_low, qkv_send = call(
        project_kernel,
        (struct((seq_dev, width), BF16), struct((group, seq_dev, 3 * LANES), BF16)),
        rows, gain1, query_weight, key_weight, value_weight,
        flops=2 * seq_dev * width * width * 3,
    )
    qkv = exchange(qkv_send, "expert").reshape(length, 3 * LANES)

    dispatch, first_t, second_t, mixed, hits, dy_send = call(
        route_kernel,
        (
            struct((slots, seq_dev), BF16),
            struct((seq_dev, slots), BF16),
            struct((seq_dev, slots), BF16),
            struct((seq_dev, LANES), F32),
            struct((seq_dev, 2 * LANES), F32),
            struct((slots, width + LANES), BF16),
        ),
        routes.reshape(seq_dev, 2), prev_pad, mix_pad, dy,
        flops=2 * slots * seq_dev * width,
    )
    qkv, dy_send = tie((qkv, dy_send))
    arrived = exchange(
        dy_send.reshape(group, most, width + LANES), "expert"
    ).reshape(slots, width + LANES)

    positions = jnp.arange(length, dtype=jnp.int32)
    starts = pieces.reshape(-1)
    inside = (positions[:, None] >= starts[None, :]) & (
        positions[:, None] < starts[None, :] + PIECE
    )
    numbers = jnp.arange(1, starts.shape[0] + 1, dtype=jnp.int32)
    labels = jnp.sum(jnp.where(inside, numbers[None, :], 0), axis=1)
    label_q = jnp.where(labels == 0, -1, labels).reshape(length // QT, QT)
    label_k = labels.reshape(length, 1)
    tiles = length // QT
    attend_flops = 54 * QT * QT * LANES * 2
    context_low, context, lse, peaks = call(
        attend_kernel,
        (
            struct((length, LANES), BF16),
            struct((length, LANES), F32),
            struct((2 * tiles, QT), F32),
            struct((2 * tiles, QT), F32),
        ),
        qkv, label_q, label_k, parity,
        scratch=(pltpu.VMEM((length, QT), F32), pltpu.VMEM((LANES, length), BF16)),
        smem=(3,),
        flops=2 * attend_flops,
    )
    context_low, arrived = tie((context_low, arrived))
    heads = exchange(context_low.reshape(group, seq_dev, LANES), "expert")
    odd = parity[0]
    pair = lax.axis_index("expert") // 2
    number = jnp.arange(HEADS, dtype=jnp.int32)
    tops = jnp.where(
        number == 3 * pair + 2 * odd,
        jnp.max(peaks[:tiles]),
        jnp.where(number == 3 * pair + 1, jnp.max(peaks[tiles:]), -jnp.inf),
    )
    head_top = lax.pmax(tops, both)
    factors = jnp.minimum(1.0, CLIP_LIMIT / head_top)
    root = jnp.repeat(jnp.sqrt(factors), HDIM)
    clipped_query = (query_weight.astype(F32) * root[None, :]).astype(BF16)
    clipped_key = (key_weight.astype(F32) * root[None, :]).astype(BF16)
    dy_rows = arrived[:, :width]
    info = arrived[:, width:].astype(F32)
    down = expert_down[0]
    hidden_back = dot_nt(dy_rows, down)

    middle, second_low, row_send = call(
        middle_kernel,
        (
            struct((seq_dev, width), F32),
            struct((seq_dev, width), BF16),
            struct((slots, width), BF16),
        ),
        rows, heads, out_weight, gain2, dispatch,
        flops=2 * seq_dev * width * 1024 + 2 * slots * seq_dev * width,
    )
    x = exchange(row_send.reshape(group, most, width), "expert").reshape(slots, width)
    first_base, second_base, partial, gate, probs, smalls = call(
        side_kernel,
        (
            struct((seq_dev, width), F32),
            struct((seq_dev, width), F32),
            struct((seq_dev, width), F32),
            struct((seq_dev, LANES), F32),
            struct((seq_dev, LANES), F32),
            struct((8, width), F32),
        ),
        second_low, dy, hits, mixed, router_pad, mixers_pad, const_vector,
        flops=4 * seq_dev * width * LANES,
    )

    x, partial, hidden_back = tie((x, partial, hidden_back))
    first_low, x = tie((first_low, x))
    first_all = lax.all_gather(first_low, "expert", axis=0, tiled=True)

    wide_gate, wide_up = expert_gate[0], expert_up[0]
    gate_act = dot_nn(x, wide_gate)
    up_act = dot_nn(x, wide_up)
    sigmoid = jax.nn.sigmoid(gate_act)
    silu = gate_act * sigmoid
    hidden = (silu * up_act).astype(BF16)
    result = dot_nn(hidden, down).astype(BF16)
    result, hidden_back = tie((result, hidden_back))
    returned = exchange(result.reshape(group, most, width), "expert").reshape(slots, width)
    gap = jnp.sum(dot_nn(x, router_weight) * info[:, :targets], axis=-1, keepdims=True)
    gap = gap + jnp.sum(info[:, 16:19], axis=-1, keepdims=True)
    share = jax.nn.sigmoid(gap)
    dy_route = (share * dy_rows.astype(F32)).astype(BF16)
    hidden_grad = share * hidden_back
    gate_low = (
        hidden_grad * up_act * sigmoid * (1.0 + gate_act * (1.0 - sigmoid))
    ).astype(BF16)
    up_low = (hidden_grad * silu).astype(BF16)
    x_grad = (dot_nt(gate_low, wide_gate) + dot_nt(up_low, wide_up)).astype(BF16)
    x_grad, x, gate_low, up_low, hidden, dy_route = tie(
        (x_grad, x, gate_low, up_low, hidden, dy_route)
    )
    x_back = exchange(x_grad.reshape(group, most, width), "expert").reshape(slots, width)
    gate_local = dot_tn(x, gate_low).astype(BF16)
    up_local = dot_tn(x, up_low).astype(BF16)
    down_local = dot_tn(hidden, dy_route).astype(BF16)
    expert_parts = [
        lax.psum_scatter(v, "dp", scatter_dimension=0, tiled=True).astype(F32)[None]
        for v in (gate_local, up_local, down_local)
    ]

    output, back, prev_grad, router_local, mix_local = call(
        output_kernel,
        (
            struct((seq_dev, width), BF16),
            struct((seq_dev, width), F32),
            struct((seq_dev, LANES), F32),
            struct((16, width), F32),
            struct((16, LANES), F32),
        ),
        returned, first_t, second_t, middle, first_base, second_base, dy, gate, probs, hits,
        second_low, router_pad, prev_pad, mix_pad, partial,
        flops=4 * slots * seq_dev * width,
    )
    middle_grad, branch_low, grad_send, gain2_local = call(
        middle_back_kernel,
        (
            struct((seq_dev, width), F32),
            struct((seq_dev, width), BF16),
            struct((group, seq_dev, LANES), BF16),
            struct((1, width), F32),
        ),
        x_back, first_t, second_t, back, middle, gain2, dy, out_weight,
        flops=2 * slots * seq_dev * width + 2 * seq_dev * width * 1024,
    )
    context_grad = exchange(grad_send, "expert").reshape(length, LANES)

    out_local = join_heads(
        lax.dot_general(
            heads, branch_low, (((1,), (0,)), ((), ())), preferred_element_type=F32
        ),
        0,
    )
    own = width // devices
    out_part = butterfly(out_local)
    context_grad, out_part = tie((context_grad, out_part))
    out_parts = exchange(out_part.astype(BF16).reshape(group, own, width), "expert")
    out_grad = jnp.sum(out_parts.astype(F32), axis=0)

    qkv_grad = call(
        attend_back_kernel,
        struct((length, 3 * LANES), BF16),
        qkv, context_grad, context, lse, label_q, label_k, parity,
        scratch=(
            pltpu.VMEM((length, LANES), F32),
            pltpu.VMEM((length, LANES), F32),
            pltpu.VMEM((length, LANES), F32),
            pltpu.VMEM((LANES, length), BF16),
        ),
        smem=(6,),
        flops=5 * attend_flops,
    )
    qkv_grad, out_grad = tie((qkv_grad, out_grad))
    home = exchange(qkv_grad.reshape(group, seq_dev, 3 * LANES), "expert")
    weight_part = butterfly(dot_tn(first_all, qkv_grad))
    home, weight_part, expert_parts = tie((home, weight_part, expert_parts))
    weight_parts = exchange(
        weight_part.astype(BF16).reshape(group, own, 3 * LANES), "expert"
    ).astype(F32)
    query_grad, key_grad, value_grad = [
        join_heads(weight_parts[:, :, part * LANES : (part + 1) * LANES], 1) for part in range(3)
    ]
    input_grad, gain1_local = call(
        input_kernel,
        (struct((seq_dev, width), F32), struct((1, width), F32)),
        home, query_weight, key_weight, value_weight, rows, gain1, middle_grad,
        flops=2 * seq_dev * width * 3072,
    )

    columns = jnp.concatenate(
        [gain1_local, gain2_local, router_local[:targets], smalls[: 3 * count]], axis=0
    )
    kinds = columns.shape[0]
    columns = columns.reshape(kinds, devices, own).transpose(1, 0, 2).reshape(devices, -1)
    shared = mix_local[:targets, :targets].T.reshape(-1)
    packed = jnp.concatenate(
        [columns, jnp.broadcast_to(shared[None], (devices, shared.size))], axis=1
    )
    size = packed.shape[1]
    packed = jnp.pad(packed, ((0, 0), (0, -size % LANES)))
    gathered = exchange(packed.reshape(devices, -1, LANES), both).reshape(devices, -1)
    summed = jnp.sum(gathered, axis=0)
    mix_grad = summed[kinds * own : size].reshape(targets, targets)
    summed = summed[: kinds * own].reshape(kinds, own)
    return (
        output.reshape(tokens.shape),
        input_grad.reshape(tokens.shape),
        prev_grad[:, :targets].reshape(prev_logits.shape),
        summed[0],
        query_grad,
        key_grad,
        value_grad,
        out_grad,
        summed[1],
        summed[2 : 2 + targets].T,
        mix_grad,
        summed[2 + targets + count : 2 + targets + 3 * count].reshape(count, 2, own),
        summed[2 + targets : 2 + targets + count],
        expert_parts[0],
        expert_parts[1],
        expert_parts[2],
        clipped_query,
        clipped_key,
        factors,
    )


def solution(mesh):
    tokens = P("dp", "expert", None)
    experts = P("expert", None, None)
    dense = P(("dp", "expert"), None)
    parts = P("expert", "dp", None)
    return jax.shard_map(
        body,
        mesh=mesh,
        in_specs=(tokens, tokens, P("dp", None), tokens, tokens)
        + (P(),) * 10
        + (experts, experts, experts),
        out_specs=(
            tokens,
            tokens,
            tokens,
            P(("dp", "expert")),
            dense,
            dense,
            dense,
            dense,
            P(("dp", "expert")),
            dense,
            P(),
            P(None, None, ("dp", "expert")),
            P(None, ("dp", "expert")),
            parts,
            parts,
            parts,
            P(),
            P(),
            P(),
        ),
        check_vma=False,
    )
```
